32 devices in a mesh: grp: 8 (over z, core), own: 4 (over y, x).
Axes of the slice: x: 2, y: 2, z: 4, core: 2. Of those that a mesh axis runs over, the one named last changes fastest.
Arguments:
- tokens: bfloat16 [8192, 1024], P(('grp', 'own')), may hold values from -6 to 6
- cotangent: bfloat16 [8192, 1024], P(('grp', 'own')), may hold values from -6 to 6
- doc_lengths: int32 [4, 4], replicated, may hold values from 256 to 1280, as said below
- w_in: float32 [1024, 3072], P('own', 'grp'), may hold values from -0.1875 to 0.1875
- w_out: float32 [1024, 1024], P('own', 'grp'), may hold values from -0.1875 to 0.1875
- w_gate: float32 [1024, 4608], P('own', 'grp'), may hold values from -0.1875 to 0.1875
- w_up: float32 [1024, 4608], P('own', 'grp'), may hold values from -0.1875 to 0.1875
- w_down: float32 [4608, 1024], P('own', 'grp'), may hold values from -0.09375 to 0.09375
- conv_w: float32 [3, 1024], P(None, 'own'), may hold values from -3.5 to 3.5
- gain: float32 [1024], P('own'), may hold values from 0.5 to 1.5
- gain_two: float32 [1024], P('own'), may hold values from 0.5 to 1.5
- moment_in: float32 [1024, 3072], P('own', 'grp'), as said below
- moment_out: float32 [1024, 1024], P('own', 'grp'), as said below
- moment_gate: float32 [1024, 4608], P('own', 'grp'), as said below
- moment_up: float32 [1024, 4608], P('own', 'grp'), as said below
- moment_down: float32 [4608, 1024], P('own', 'grp'), as said below
- moment_conv: float32 [3, 1024], P(None, 'own'), as said below
- moment_gain: float32 [1024], P('own'), as said below
- moment_gain_two: float32 [1024], P('own'), as said below
- square_in: float32 [1024, 3072], P('own', 'grp'), as said below
- square_out: float32 [1024, 1024], P('own', 'grp'), as said below
- square_gate: float32 [1024, 4608], P('own', 'grp'), as said below
- square_up: float32 [1024, 4608], P('own', 'grp'), as said below
- square_down: float32 [4608, 1024], P('own', 'grp'), as said below
- square_conv: float32 [3, 1024], P(None, 'own'), as said below
- square_gain: float32 [1024], P('own'), as said below
- square_gain_two: float32 [1024], P('own'), as said below
Outputs:
- block_out: bfloat16 [8192, 1024], P(('grp', 'own'))
- grad_tokens: bfloat16 [8192, 1024], P(('grp', 'own'))
- grad_w_in: float32 [1024, 3072], P('own')
- grad_w_out: float32 [1024, 1024], P('own')
- grad_w_gate: float32 [1024, 4608], P('own')
- grad_w_up: float32 [1024, 4608], P('own')
- grad_w_down: float32 [4608, 1024], P('own')
- grad_conv_w: float32 [3, 1024], P(None, 'own')
- grad_gain: float32 [1024], P('own')
- grad_gain_two: float32 [1024], P('own')
- new_w_in: float32 [1024, 3072], P('own', 'grp')
- new_w_out: float32 [1024, 1024], P('own', 'grp')
- new_w_gate: float32 [1024, 4608], P('own', 'grp')
- new_w_up: float32 [1024, 4608], P('own', 'grp')
- new_w_down: float32 [4608, 1024], P('own', 'grp')
- new_conv_w: float32 [3, 1024], P(None, 'own')
- new_gain: float32 [1024], P('own')
- new_gain_two: float32 [1024], P('own')
- new_moment_in: float32 [1024, 3072], P('own', 'grp')
- new_moment_out: float32 [1024, 1024], P('own', 'grp')
- new_moment_gate: float32 [1024, 4608], P('own', 'grp')
- new_moment_up: float32 [1024, 4608], P('own', 'grp')
- new_moment_down: float32 [4608, 1024], P('own', 'grp')
- new_moment_conv: float32 [3, 1024], P(None, 'own')
- new_moment_gain: float32 [1024], P('own')
- new_moment_gain_two: float32 [1024], P('own')
- new_square_in: float32 [1024, 3072], P('own', 'grp')
- new_square_out: float32 [1024, 1024], P('own', 'grp')
- new_square_gate: float32 [1024, 4608], P('own', 'grp')
- new_square_up: float32 [1024, 4608], P('own', 'grp')
- new_square_down: float32 [4608, 1024], P('own', 'grp')
- new_square_conv: float32 [3, 1024], P(None, 'own')
- new_square_gain: float32 [1024], P('own')
- new_square_gain_two: float32 [1024], P('own')
The draws below stay inside these ranges and needn't reach their ends.
Inputs may be any that keep to these rules, and one draw needn't show every extreme that they name: `doc_lengths`: the 4 lengths of each sequence sum to 2048. `moment_in`: first moments: real values of either sign. `moment_out`: first moments: real values of either sign. `moment_gate`: first moments: real values of either sign. `moment_up`: first moments: real values of either sign. `moment_down`: first moments: real values of either sign. `moment_conv`: first moments: real values of either sign. `moment_gain`: first moments: real values of either sign. `moment_gain_two`: first moments: real values of either sign. `square_in`: second moments are positive. `square_out`: second moments are positive. `square_gate`: second moments are positive. `square_up`: second moments are positive. `square_down`: second moments are positive. `square_conv`: second moments are positive. `square_gain`: second moments are positive. `square_gain_two`: second moments are positive.
All inputs are finite; a program needn't handle non-finite values.
Results may differ from the reference program's by a relative error of at most 0.025.
Values may be sent and summed in bfloat16 or wider, within the bound.
No kernel may reach another device: no remote copies, remote signals or barrier semaphores. Data moves between devices by JAX's collectives and lax.ppermute only.
A program may use at most 320 MiB of HBM per device.

```python
import jax
import jax.numpy as jnp
from jax import lax

D = 1024
FF = 4608
TAPS = 3
SEQ_LEN = 2048
DOCS = 4
MIN_DOC = 256
TOKENS = 8192
SEQS = 4


def draw_doc_lengths(key, part):
    spare = SEQ_LEN - DOCS * MIN_DOC
    cuts = jnp.sort(jax.random.randint(key, (SEQS, DOCS - 1), 0, spare + 1, dtype=jnp.int32), axis=1)
    first_row = (jnp.arange(SEQS, dtype=jnp.int32) == 0)[:, None]
    cuts = jnp.where(first_row, 0, cuts)
    edges = jnp.concatenate([jnp.zeros((SEQS, 1), jnp.int32), cuts, jnp.full((SEQS, 1), spare, jnp.int32)], 1)
    return (edges[:, 1:] - edges[:, :-1] + MIN_DOC).astype(jnp.int32)


def first_moment(key, shape, label):
    key = jax.random.fold_in(key, label)
    values = jnp.clip(jax.random.normal(key, shape, jnp.float32), -4.0, 4.0)
    return values * (0.1 * jnp.sqrt(jnp.float32(TOKENS)))


def second_moment(key, shape, label):
    key = jax.random.fold_in(key, label)
    values = jnp.exp(jax.random.uniform(key, shape, jnp.float32, jnp.log(0.01), jnp.log(0.1)))
    return values * jnp.float32(TOKENS)


def draw_moment_in(key, part):
    return first_moment(key, (D, 3 * D), 11)


def draw_moment_out(key, part):
    return first_moment(key, (D, D), 12)


def draw_moment_gate(key, part):
    return first_moment(key, (D, FF), 13)


def draw_moment_up(key, part):
    return first_moment(key, (D, FF), 14)


def draw_moment_down(key, part):
    return first_moment(key, (FF, D), 15)


def draw_moment_conv(key, part):
    return first_moment(key, (TAPS, D), 16)


def draw_moment_gain(key, part):
    return first_moment(key, (D,), 17)


def draw_moment_gain_two(key, part):
    return first_moment(key, (D,), 18)


def draw_square_in(key, part):
    return second_moment(key, (D, 3 * D), 21)


def draw_square_out(key, part):
    return second_moment(key, (D, D), 22)


def draw_square_gate(key, part):
    return second_moment(key, (D, FF), 23)


def draw_square_up(key, part):
    return second_moment(key, (D, FF), 24)


def draw_square_down(key, part):
    return second_moment(key, (FF, D), 25)


def draw_square_conv(key, part):
    return second_moment(key, (TAPS, D), 26)


def draw_square_gain(key, part):
    return second_moment(key, (D,), 27)


def draw_square_gain_two(key, part):
    return second_moment(key, (D,), 28)


def steps_of(own_key, shape, split, smallest, largest):
    level, own = 1.0, jax.random.fold_in(own_key, 6)
    for dim, blocks in split:
        steps = jnp.exp(jax.random.uniform(jax.random.fold_in(own, dim), (blocks,), jnp.float32, smallest / len(split), largest / len(split)))
        level = level * jnp.repeat(steps, shape[dim] // blocks).reshape([-1 if axis == dim else 1 for axis in range(len(shape))])
    return level


def centred(own_key, shape, width, bound, pieces=(), kind=jnp.bfloat16):
    values = width * jax.random.normal(own_key, shape, jnp.float32)
    if pieces:
        values = values * steps_of(own_key, shape, pieces, -0.22, 0.18)
    return jnp.clip(values, -bound, bound).astype(kind)


def setup_inputs(seed: int = 0) -> dict:
    key_list = jax.random.split(jax.random.key(seed), 28)
    return {
        "tokens": centred(key_list[0], (TOKENS, D), 1.0, 6.0, ((0, 32),)),
        "cotangent": centred(key_list[1], (TOKENS, D), 1.0, 6.0, ((0, 32),)),
        "doc_lengths": draw_doc_lengths(jax.random.fold_in(key_list[27], 71), 0),
        "w_in": centred(key_list[3], (D, 3 * D), D ** -0.5, 0.1875, ((0, 4), (1, 8)), jnp.float32),
        "w_out": centred(key_list[4], (D, D), D ** -0.5, 0.1875, ((0, 4), (1, 8)), jnp.float32),
        "w_gate": centred(key_list[5], (D, FF), D ** -0.5, 0.1875, ((0, 4), (1, 8)), jnp.float32),
        "w_up": centred(key_list[6], (D, FF), D ** -0.5, 0.1875, ((0, 4), (1, 8)), jnp.float32),
        "w_down": centred(key_list[7], (FF, D), FF ** -0.5, 0.09375, ((0, 4), (1, 8)), jnp.float32),
        "conv_w": centred(key_list[8], (TAPS, D), TAPS ** -0.5, 3.5, ((1, 4),), jnp.float32),
        "gain": jnp.clip(1.0 + 0.1 * jax.random.normal(key_list[9], (D,), jnp.float32), 0.5, 1.5),
        "gain_two": jnp.clip(1.0 + 0.1 * jax.random.normal(key_list[10], (D,), jnp.float32), 0.5, 1.5),
        "moment_in": draw_moment_in(jax.random.fold_in(key_list[27], 71), 0),
        "moment_out": draw_moment_out(jax.random.fold_in(key_list[27], 71), 0),
        "moment_gate": draw_moment_gate(jax.random.fold_in(key_list[27], 71), 0),
        "moment_up": draw_moment_up(jax.random.fold_in(key_list[27], 71), 0),
        "moment_down": draw_moment_down(jax.random.fold_in(key_list[27], 71), 0),
        "moment_conv": draw_moment_conv(jax.random.fold_in(key_list[27], 71), 0),
        "moment_gain": draw_moment_gain(jax.random.fold_in(key_list[27], 71), 0),
        "moment_gain_two": draw_moment_gain_two(jax.random.fold_in(key_list[27], 71), 0),
        "square_in": draw_square_in(jax.random.fold_in(key_list[27], 71), 0),
        "square_out": draw_square_out(jax.random.fold_in(key_list[27], 71), 0),
        "square_gate": draw_square_gate(jax.random.fold_in(key_list[27], 71), 0),
        "square_up": draw_square_up(jax.random.fold_in(key_list[27], 71), 0),
        "square_down": draw_square_down(jax.random.fold_in(key_list[27], 71), 0),
        "square_conv": draw_square_conv(jax.random.fold_in(key_list[27], 71), 0),
        "square_gain": draw_square_gain(jax.random.fold_in(key_list[27], 71), 0),
        "square_gain_two": draw_square_gain_two(jax.random.fold_in(key_list[27], 71), 0),
    }


eps_norm = 1e-05
eps_adam = 1e-08
beta_one = 0.9
beta_two = 0.95
train_step = 5
rate_matrix = 0.004
rate_vector = 0.1
decay_matrix = 0.1

def stream_starts(doc_lengths, seq_len):
    starts = (jnp.cumsum(doc_lengths, axis=1) - doc_lengths).astype(jnp.int32)
    base = (jnp.arange(doc_lengths.shape[0], dtype=jnp.int32) * seq_len)[:, None]
    first = (jnp.arange(doc_lengths.shape[1], dtype=jnp.int32) == 0)[None, :]
    return jnp.where(first, 0, base + starts).astype(jnp.int32).reshape(-1)

def since_start(positions, stream):
    below = jnp.where(stream[None, :] <= positions[:, None], stream[None, :], 0)
    return (positions - lax.optimization_barrier(jnp.max(below, axis=1))).astype(jnp.int32)

def apply_adam(param, first, second, grad, rate, decay):
    first_new = beta_one * first + (1.0 - beta_one) * grad
    second_new = beta_two * second + (1.0 - beta_two) * grad * grad
    first_hat = first_new / (1.0 - beta_one ** train_step)
    second_hat = second_new / (1.0 - beta_two ** train_step)
    param_new = param - rate * (first_hat / (jnp.sqrt(second_hat) + eps_adam) + decay * param)
    return (param_new, first_new, second_new)

def reference(tokens, cotangent, doc_lengths, w_in, w_out, w_gate, w_up, w_down, conv_w, gain, gain_two, moment_in, moment_out, moment_gate, moment_up, moment_down, moment_conv, moment_gain, moment_gain_two, square_in, square_out, square_gate, square_up, square_down, square_conv, square_gain, square_gain_two):
    in_half = w_in.astype(jnp.bfloat16)
    out_half = w_out.astype(jnp.bfloat16)
    gate_half = w_gate.astype(jnp.bfloat16)
    up_half = w_up.astype(jnp.bfloat16)
    down_half = w_down.astype(jnp.bfloat16)
    conv_float = lax.optimization_barrier(conv_w.astype(jnp.bfloat16)).astype(jnp.float32)
    gain_float = lax.optimization_barrier(gain.astype(jnp.bfloat16)).astype(jnp.float32)
    gain_two_float = lax.optimization_barrier(gain_two.astype(jnp.bfloat16)).astype(jnp.float32)
    pair = 2 if SEQS % 2 == 0 else 1
    span = pair * SEQ_LEN
    blocks = TOKENS // span
    rim = TAPS - 1
    window = span + 2 * rim
    stream = stream_starts(doc_lengths, SEQ_LEN)
    padding = jnp.zeros((rim, D), jnp.bfloat16)
    tokens_pad = jnp.concatenate([padding, tokens, padding], 0)
    cot_pad = jnp.concatenate([padding, cotangent, padding], 0)

    def one_block(carry, block_index):
        head = (block_index * span).astype(jnp.int32)
        token_block = lax.dynamic_slice_in_dim(tokens_pad, head, window, 0)
        cot_block = lax.dynamic_slice_in_dim(cot_pad, head, window, 0)
        glob = head - rim + jnp.arange(window, dtype=jnp.int32)
        valid = ((glob >= 0) & (glob < TOKENS))[:, None]
        since = since_start(glob, stream)
        x_float = token_block.astype(jnp.float32)
        cot_float = cot_block.astype(jnp.float32)
        inv_rms = lax.rsqrt(lax.optimization_barrier(jnp.mean(x_float * x_float, axis=1, keepdims=True)) + eps_norm)
        normed = (x_float * inv_rms * gain_float).astype(jnp.bfloat16)
        project = jnp.dot(normed, in_half, preferred_element_type=jnp.float32)
        b_gate = project[:, :D]
        c_gate = project[:, D:2 * D]
        x_value = project[:, 2 * D:]
        gated = b_gate * x_value
        convolved = jnp.zeros((window, D), jnp.float32)
        for tap_index in range(TAPS):
            moved = jnp.concatenate([jnp.zeros((tap_index, D), jnp.float32), gated[:window - tap_index]], 0)
            keep = (since >= tap_index)[:, None]
            convolved = convolved + jnp.where(keep, conv_float[tap_index] * moved, 0.0)
        mixed = (c_gate * convolved).astype(jnp.bfloat16)
        middle = x_float + jnp.dot(mixed, out_half, preferred_element_type=jnp.float32)
        inv_two = lax.rsqrt(lax.optimization_barrier(jnp.mean(middle * middle, axis=1, keepdims=True)) + eps_norm)
        normed_two = (middle * inv_two * gain_two_float).astype(jnp.bfloat16)
        gate = jnp.dot(normed_two, gate_half, preferred_element_type=jnp.float32)
        up = jnp.dot(normed_two, up_half, preferred_element_type=jnp.float32)
        sig = jax.nn.sigmoid(gate)
        activated = gate * sig
        hidden = (activated * up).astype(jnp.bfloat16)
        block_out = (middle + jnp.dot(hidden, down_half, preferred_element_type=jnp.float32)).astype(jnp.bfloat16)
        grad_hidden = jnp.dot(cot_block, down_half.T, preferred_element_type=jnp.float32)
        grad_gate = (grad_hidden * up * sig * (1.0 + gate * (1.0 - sig))).astype(jnp.bfloat16)
        grad_up = (grad_hidden * activated).astype(jnp.bfloat16)
        grad_normed_two = jnp.dot(grad_gate, gate_half.T, preferred_element_type=jnp.float32) + jnp.dot(grad_up, up_half.T, preferred_element_type=jnp.float32)
        weighted_two = gain_two_float * grad_normed_two
        grad_middle = cot_float + inv_two * weighted_two - middle * inv_two * inv_two * inv_two * lax.optimization_barrier(jnp.mean(weighted_two * middle, axis=1, keepdims=True))
        grad_middle_half = grad_middle.astype(jnp.bfloat16)
        grad_mixed = jnp.dot(grad_middle_half, out_half.T, preferred_element_type=jnp.float32)
        grad_c = grad_mixed * convolved
        grad_conv = jnp.where(valid, grad_mixed * c_gate, 0.0)
        grad_gated = jnp.zeros((window, D), jnp.float32)
        tap_sums = []
        for tap_index in range(TAPS):
            keep = (since >= tap_index)[:, None]
            kept = jnp.where(keep, grad_conv, 0.0)
            ahead = jnp.concatenate([kept[tap_index:], jnp.zeros((tap_index, D), jnp.float32)], 0)
            grad_gated = grad_gated + conv_float[tap_index] * ahead
            moved = jnp.concatenate([jnp.zeros((tap_index, D), jnp.float32), gated[:window - tap_index]], 0)
            tap_sums.append(lax.optimization_barrier(jnp.sum(jnp.where(keep, grad_conv * moved, 0.0)[rim:rim + span], axis=0)))
        own = slice(rim, rim + span)
        grad_b = grad_gated[own] * x_value[own]
        grad_x = grad_gated[own] * b_gate[own]
        grad_project = jnp.concatenate([grad_b, grad_c[own], grad_x], 1).astype(jnp.bfloat16)
        grad_normed = jnp.dot(grad_project, in_half.T, preferred_element_type=jnp.float32)
        x_own = x_float[own]
        inv_own = inv_rms[own]
        grad_gain = lax.optimization_barrier(jnp.sum(grad_normed * x_own * inv_own, axis=0))
        grad_gain_two = lax.optimization_barrier(jnp.sum((grad_normed_two * middle * inv_two)[own], axis=0))
        weighted = gain_float * grad_normed
        grad_tokens = (grad_middle[own] + inv_own * weighted - x_own * inv_own * inv_own * inv_own * lax.optimization_barrier(jnp.mean(weighted * x_own, axis=1, keepdims=True))).astype(jnp.bfloat16)
        grad_in_w = jnp.dot(normed[own].T, grad_project, preferred_element_type=jnp.float32)
        grad_out_w = jnp.dot(mixed[own].T, grad_middle_half[own], preferred_element_type=jnp.float32)
        grad_gate_w = jnp.dot(normed_two[own].T, grad_gate[own], preferred_element_type=jnp.float32)
        grad_up_w = jnp.dot(normed_two[own].T, grad_up[own], preferred_element_type=jnp.float32)
        grad_down_w = jnp.dot(hidden[own].T, cot_block[own], preferred_element_type=jnp.float32)
        grad_taps = jnp.stack(tap_sums, 0)
        total = carry
        carry = (total[0] + grad_in_w, total[1] + grad_out_w, total[2] + grad_gate_w, total[3] + grad_up_w, total[4] + grad_down_w, total[5] + grad_taps, total[6] + grad_gain, total[7] + grad_gain_two)
        return (carry, (block_out[own], grad_tokens))
    start = (jnp.zeros((D, 3 * D), jnp.float32), jnp.zeros((D, D), jnp.float32), jnp.zeros((D, FF), jnp.float32), jnp.zeros((D, FF), jnp.float32), jnp.zeros((FF, D), jnp.float32), jnp.zeros((TAPS, D), jnp.float32), jnp.zeros((D,), jnp.float32), jnp.zeros((D,), jnp.float32))
    sums, outputs = lax.scan(one_block, start, jnp.arange(blocks, dtype=jnp.int32))
    grad_w_in, grad_w_out, grad_w_gate, grad_w_up, grad_w_down, grad_conv_w, grad_gain, grad_gain_two = sums
    block_out = outputs[0].reshape(TOKENS, D)
    grad_tokens = outputs[1].reshape(TOKENS, D)
    new_w_in, new_moment_in, new_square_in = apply_adam(w_in, moment_in, square_in, grad_w_in, rate_matrix, decay_matrix)
    new_w_out, new_moment_out, new_square_out = apply_adam(w_out, moment_out, square_out, grad_w_out, rate_matrix, decay_matrix)
    new_w_gate, new_moment_gate, new_square_gate = apply_adam(w_gate, moment_gate, square_gate, grad_w_gate, rate_matrix, decay_matrix)
    new_w_up, new_moment_up, new_square_up = apply_adam(w_up, moment_up, square_up, grad_w_up, rate_matrix, decay_matrix)
    new_w_down, new_moment_down, new_square_down = apply_adam(w_down, moment_down, square_down, grad_w_down, rate_matrix, decay_matrix)
    new_conv_w, new_moment_conv, new_square_conv = apply_adam(conv_w, moment_conv, square_conv, grad_conv_w, rate_vector, 0.0)
    new_gain, new_moment_gain, new_square_gain = apply_adam(gain, moment_gain, square_gain, grad_gain, rate_vector, 0.0)
    new_gain_two, new_moment_gain_two, new_square_gain_two = apply_adam(gain_two, moment_gain_two, square_gain_two, grad_gain_two, rate_vector, 0.0)
    return (block_out, grad_tokens, grad_w_in, grad_w_out, grad_w_gate, grad_w_up, grad_w_down, grad_conv_w, grad_gain, grad_gain_two, new_w_in, new_w_out, new_w_gate, new_w_up, new_w_down, new_conv_w, new_gain, new_gain_two, new_moment_in, new_moment_out, new_moment_gate, new_moment_up, new_moment_down, new_moment_conv, new_moment_gain, new_moment_gain_two, new_square_in, new_square_out, new_square_gate, new_square_up, new_square_down, new_square_conv, new_square_gain, new_square_gain_two)
```

```python
import jax
import jax.numpy as jnp
from jax import lax
from jax.sharding import PartitionSpec as P


SEQ_LEN = 2048


eps_norm = 1e-05
eps_adam = 1e-08
beta_one = 0.9
beta_two = 0.95
train_step = 5
rate_matrix = 0.004
rate_vector = 0.1
decay_matrix = 0.1

half = jnp.bfloat16
full = jnp.float32


def exchange(block, k):
    devices = range(lax.axis_size("own"))
    return lax.ppermute(block, "own", [(i, i ^ k) for i in devices])


def gather_own(block):
    places = range(1, lax.axis_size("own"))
    arrived = [exchange(block, k) for k in places]
    return jnp.concatenate([block] + arrived, 0)


def scatter_own(part_of):
    places = range(1, lax.axis_size("own"))
    arrived = []
    for k in places:
        part = part_of(k).astype(half)
        arrived.append(exchange(part, k))
    total = part_of(0)
    for block in arrived:
        total = total + block.astype(full)
    return total


def passed_along(block, distance):
    devices = range(lax.axis_size("grp"))
    route = [(i - distance, i) for i in devices if i - distance in devices]
    return lax.ppermute(block, "grp", route)


def exchange_core(block):
    devices = range(lax.axis_size("grp"))
    return lax.ppermute(block, "grp", [(i, i ^ 1) for i in devices])


class Line:

    def __init__(self, array):
        self.chips = lax.axis_size("grp") // 2
        self.array = array
        self.total = 0.0
        self.arrived = None
        self.step = 1

    def going(self):
        return self.step < self.chips

    def hop(self):
        chips, step = self.chips, self.step
        hops = [(step - 1, step), (chips - step, chips - 1 - step)]
        route = [(2 * a + core, 2 * b + core) for a, b in hops for core in range(2)]
        sent = self.array if step == 1 else self.array + self.arrived
        return lax.ppermute(sent, "grp", route)

    def take(self, arrived):
        self.arrived = arrived
        self.total = self.total + arrived.astype(full)
        self.step += 1

    def sum(self):
        return (self.array.astype(full) + self.total).astype(half)


def tick(lines, beside):
    lines = [line for line in lines if line.going()]
    hops = [line.hop() for line in lines]
    hops, beside = lax.optimization_barrier((hops, beside))
    for line, arrived in zip(lines, hops):
        line.take(arrived)
    return beside


def swap_own(pieces):
    return lax.all_to_all(pieces, "own", 0, 0, tiled=True)


def stream_starts(doc_lengths, seq_len):
    starts = jnp.cumsum(doc_lengths, axis=1) - doc_lengths
    base = (jnp.arange(doc_lengths.shape[0], dtype=jnp.int32) * seq_len)[:, None]
    first = (jnp.arange(doc_lengths.shape[1], dtype=jnp.int32) == 0)[None, :]
    return jnp.where(first, 0, base + starts).reshape(-1)


def since_start(positions, stream):
    below = jnp.where(stream[None, :] <= positions[:, None], stream[None, :], 0)
    return positions - jnp.max(below, axis=1)


def apply_adam(param, first, second, grad, rate, decay):
    first_new = beta_one * first + (1.0 - beta_one) * grad
    second_new = beta_two * second + (1.0 - beta_two) * grad * grad
    first_hat = first_new / (1.0 - beta_one**train_step)
    second_hat = second_new / (1.0 - beta_two**train_step)
    param_new = param - rate * (first_hat / (jnp.sqrt(second_hat) + eps_adam) + decay * param)
    return (param_new, first_new, second_new)


def dot(left, right):
    return jnp.dot(left, right, preferred_element_type=full)


def dot_rows(left, right):
    return lax.dot_general(left, right, (((1,), (1,)), ((), ())), preferred_element_type=full)


def dot_tokens(left, right):
    return lax.dot_general(left, right, (((0,), (0,)), ((), ())), preferred_element_type=full)


def pick(index, blocks):
    total = jnp.zeros_like(blocks[0])
    for place, block in enumerate(blocks):
        total = jnp.where(index == place, block, total)
    return total


def local(
    tokens,
    cotangent,
    doc_lengths,
    w_in,
    w_out,
    w_gate,
    w_up,
    w_down,
    conv_w,
    gain,
    gain_two,
    moment_in,
    moment_out,
    moment_gate,
    moment_up,
    moment_down,
    moment_conv,
    moment_gain,
    moment_gain_two,
    square_in,
    square_out,
    square_gate,
    square_up,
    square_down,
    square_conv,
    square_gain,
    square_gain_two,
):
    groups = lax.axis_size("grp")
    owners = lax.axis_size("own")
    group = lax.axis_index("grp")
    owner = lax.axis_index("own")
    rows, width = tokens.shape
    taps = conv_w.shape[0]
    rim = taps - 1
    channels = width // owners
    sub = width // (groups * owners)
    run = w_gate.shape[1] * groups // owners
    share = groups // owners
    thin = w_out.shape[1]

    def columns_for(matrix, pieces):
        cut = matrix.astype(half).T.reshape(pieces, owners, -1, channels)
        return cut.transpose(1, 0, 2, 3).reshape(owners, -1, channels)

    def rows_for(matrix):
        cut = matrix.astype(half).reshape(share, owners, -1, thin)
        return cut.transpose(1, 2, 0, 3).reshape(owners, -1, channels)

    def columns_from(pieces):
        return pieces.transpose(1, 0, 2).reshape(-1, width)

    def rows_gathered(blocks):
        cut = blocks.reshape(groups, -1, groups, thin)
        return cut.transpose(2, 1, 0, 3).reshape(-1, width)

    small = jnp.concatenate([conv_w, gain[None], gain_two[None]], 0).astype(half)
    small = jnp.broadcast_to(small[None], (owners,) + small.shape)
    small_rows = small.shape[1]
    first = jnp.concatenate([columns_for(w_in, 3), rows_for(w_out), small], 1)
    first = swap_own(first)
    tokens_late, first = lax.optimization_barrier((tokens, first))
    x_half = gather_own(tokens_late)
    split = 3 * sub
    small = first[:, split + sub :].transpose(1, 0, 2).reshape(small_rows, width).astype(full)
    first = lax.all_gather(columns_from(first[:, : split + sub]), "grp", axis=0, tiled=False)
    in_t = first[:, :split].reshape(3 * channels, width)
    out_half = rows_gathered(first[:, split:])
    conv_all = small[:taps].reshape(taps, groups, owners, sub)
    conv_float = lax.dynamic_index_in_dim(conv_all, owner, 2, False).reshape(taps, channels)
    gain_float = small[taps]
    gain_two_float = small[taps + 1]
    second = jnp.concatenate([columns_for(w_gate, 1), columns_for(w_up, 1), rows_for(w_down)], 1)
    piece = run // groups
    second = swap_own(second)
    second = lax.all_gather(columns_from(second), "grp", axis=0, tiled=False)
    gate_t = second[:, :piece].reshape(run, width)
    up_t = second[:, piece : 2 * piece].reshape(run, width)
    down_half = rows_gathered(second[:, 2 * piece :])
    cot_late, x_half = lax.optimization_barrier((cotangent, x_half))
    cot_half = gather_own(cot_late)

    places = [owner ^ k for k in range(owners)]
    stream = stream_starts(doc_lengths, SEQ_LEN)
    line = jnp.arange(rows, dtype=jnp.int32)
    position = jnp.concatenate([(group * owners + place) * rows + line for place in places])
    since = since_start(position, stream).reshape(owners, rows, 1)

    x_all = x_half.astype(full)
    inv_all = lax.rsqrt(jnp.mean(x_all * x_all, axis=1, keepdims=True) + eps_norm)
    normed = (x_all * inv_all * gain_float).astype(half)
    project = dot_rows(normed, in_t)
    b_gate = project[:, :channels].reshape(owners, rows, channels)
    c_gate = project[:, channels : 2 * channels].reshape(owners, rows, channels)
    x_value = project[:, 2 * channels :].reshape(owners, rows, channels)
    gated = b_gate * x_value
    tails = [gated[k, rows - rim :] for k in range(owners)]
    last_tail = pick((owners - 1) ^ owner, tails)
    before_group = passed_along(last_tail, 1)
    before = jnp.stack(
        [
            jnp.where(place == 0, before_group, pick((place - 1) ^ owner, tails))
            for place in places
        ]
    )
    extended = jnp.concatenate([before, gated], 1)

    def moved(tap):
        return extended[:, rim - tap : rim - tap + rows]

    convolved = conv_float[0] * gated
    for tap in range(1, taps):
        convolved = convolved + jnp.where(since >= tap, conv_float[tap] * moved(tap), 0.0)
    mixed = (c_gate * convolved).astype(half)
    x_float = tokens.astype(full)
    middle = x_float + scatter_own(lambda k: dot(mixed[k], out_half))
    inv_two = lax.rsqrt(jnp.mean(middle * middle, axis=1, keepdims=True) + eps_norm)
    normed_two = gather_own((middle * inv_two * gain_two_float).astype(half))
    gate = dot_rows(normed_two, gate_t)
    up = dot_rows(normed_two, up_t)
    sig = jax.nn.sigmoid(gate)
    activated = gate * sig
    hidden = (activated * up).astype(half)
    core = group % 2

    def core_half(array, axis):
        count = array.shape[axis] // 2
        keep = lax.dynamic_slice_in_dim(array, core * count, count, axis)
        send = lax.dynamic_slice_in_dim(array, (1 - core) * count, count, axis)
        return (keep.astype(full) + exchange_core(send).astype(full)).astype(half)

    def owner_blocks(array, axis):
        count = array.shape[axis] // owners
        return [
            lax.dynamic_slice_in_dim(array, (owner ^ k) * count, count, axis)
            for k in range(owners)
        ]

    def to_owner(blocks):
        return [blocks[0]] + [exchange(blocks[k], k) for k in range(1, owners)]

    def both_cores(blocks):
        mine = jnp.stack([pick(place ^ owner, blocks) for place in range(owners)])
        other = exchange_core(mine)
        low = jnp.where(core == 0, mine, other)
        high = jnp.where(core == 0, other, mine)
        return low, high

    def join_columns(halves, count):
        both = jnp.concatenate(halves, 1).reshape(owners, -1, count, channels)
        return both.transpose(1, 0, 2, 3).reshape(-1, channels)

    def join_rows(halves, count):
        both = jnp.concatenate(halves, 2).reshape(owners, share, count, width)
        return both.transpose(1, 0, 2, 3).reshape(-1, width)

    down_part = dot_tokens(hidden, cot_half).astype(half)
    gate, up, down_part = lax.optimization_barrier((gate, up, down_part))
    sig = jax.nn.sigmoid(gate)
    activated = gate * sig
    down_line = Line(core_half(down_part, 1))
    grad_hidden = dot_rows(cot_half, down_half)
    grad_gate = (grad_hidden * up * sig * (1.0 + gate * (1.0 - sig))).astype(half)
    grad_up = (grad_hidden * activated).astype(half)

    def block(array, k):
        return array[k * rows : (k + 1) * rows]

    gate_part = dot_tokens(grad_gate, normed_two).astype(half)
    gate_line = Line(core_half(gate_part, 0))
    up_part = dot_tokens(grad_up, normed_two).astype(half)
    up_line = Line(core_half(up_part, 0))

    grad_normed_two = scatter_own(
        lambda k: dot(block(grad_gate, k), gate_t) + dot(block(grad_up, k), up_t),
    )
    grad_normed_two, gate_line.array = tick([down_line], (grad_normed_two, gate_line.array))
    gain_two_rows = jnp.sum(grad_normed_two * middle * inv_two, axis=0)
    weighted_two = gain_two_float * grad_normed_two
    grad_middle = (
        cotangent.astype(full)
        + inv_two * weighted_two
        - middle
        * inv_two
        * inv_two
        * inv_two
        * jnp.mean(weighted_two * middle, axis=1, keepdims=True)
    )
    grad_middle_half = gather_own(grad_middle.astype(half))
    grad_middle_half, up_line.array, hidden_late = tick(
        [down_line, gate_line], (grad_middle_half, up_line.array, hidden)
    )
    grad_mixed = dot_rows(grad_middle_half, out_half).reshape(owners, rows, channels)
    grad_c = grad_mixed * convolved
    grad_conv = grad_mixed * c_gate
    tap_sums = [jnp.sum(grad_conv * gated, axis=(0, 1))]
    grad_gated = conv_float[0] * grad_conv
    kept = [jnp.where(since >= tap, grad_conv, 0.0) for tap in range(1, taps)]
    heads = [
        jnp.concatenate([kept[tap - 1][k, :tap] for tap in range(1, taps)], 0)
        for k in range(owners)
    ]
    after_group = passed_along(pick(owner, heads), -1)
    after = jnp.stack(
        [
            jnp.where(place == owners - 1, after_group, pick((place + 1) ^ owner, heads))
            for place in places
        ]
    )
    line = 0
    for tap in range(1, taps):
        ahead = jnp.concatenate([kept[tap - 1][:, tap:], after[:, line : line + tap]], 1)
        line = line + tap
        grad_gated = grad_gated + conv_float[tap] * ahead
        tap_sums.append(jnp.sum(kept[tap - 1] * moved(tap), axis=(0, 1)))
    grad_project = (
        jnp.concatenate([grad_gated * x_value, grad_c, grad_gated * b_gate], 2)
        .astype(half)
        .reshape(owners * rows, 3 * channels)
    )
    in_part = core_half(dot_tokens(grad_project, normed).astype(half), 0)
    out_part = core_half(
        dot_tokens(mixed.reshape(owners * rows, channels), grad_middle_half).astype(half), 1
    )
    in_rows, out_rows = in_part.shape[0], out_part.shape[0] // 2
    out_part = jnp.concatenate([out_part[:out_rows], out_part[out_rows:]], 1)
    last_line = Line(jnp.concatenate([in_part, out_part], 0))
    feed_out = scatter_own(lambda k: dot(block(hidden_late, k), down_half))
    block_out = (middle + feed_out).astype(half)
    last_line.array, block_out, project_late = tick(
        [down_line, gate_line, up_line], (last_line.array, block_out, grad_project)
    )
    grad_normed = scatter_own(lambda k: dot(block(project_late, k), in_t))

    piece = run // groups
    while down_line.going():
        tick([down_line, gate_line, up_line, last_line], ())
    down_blocks = to_owner(owner_blocks(down_line.sum(), 0))
    down_blocks = tick([gate_line, up_line, last_line], down_blocks)
    gate_blocks = to_owner(owner_blocks(gate_line.sum(), 1))
    down_grad = join_rows(both_cores(down_blocks), piece)
    gate_blocks, down_grad, grad_normed = tick(
        [up_line, last_line], (gate_blocks, down_grad, grad_normed)
    )
    inv_rms = lax.rsqrt(jnp.mean(x_float * x_float, axis=1, keepdims=True) + eps_norm)
    gain_rows = jnp.sum(grad_normed * x_float * inv_rms, axis=0)
    weighted = gain_float * grad_normed
    grad_tokens = (
        grad_middle
        + inv_rms * weighted
        - x_float
        * inv_rms
        * inv_rms
        * inv_rms
        * jnp.mean(weighted * x_float, axis=1, keepdims=True)
    ).astype(half)
    tap_pieces = jnp.stack(tap_sums).reshape(taps, owners, share * sub).transpose(1, 0, 2)
    tap_pieces = jnp.pad(tap_pieces, ((0, 0), (0, 0), (0, channels - share * sub)))
    gain_pieces = jnp.stack([gain_rows, gain_two_rows]).reshape(2, owners, channels)
    pieces = jnp.concatenate([tap_pieces, gain_pieces.transpose(1, 0, 2)], 1)
    pieces = swap_own(pieces)
    tap_share = pieces[:, :taps, : share * sub].reshape(owners, taps, share, sub)
    tap_share = tap_share.transpose(1, 2, 0, 3).reshape(taps, channels)
    gain_share = jnp.sum(pieces[:, taps:], axis=0)
    small_share = jnp.concatenate([tap_share, gain_share], 0)

    up_blocks = to_owner(owner_blocks(up_line.sum(), 1))
    gate_grad = join_columns(both_cores(gate_blocks), piece)
    down_shard = lax.dynamic_slice_in_dim(down_grad, group * thin, thin, 1)
    down_new = apply_adam(
        w_down, moment_down, square_down, down_shard.astype(full), rate_matrix, decay_matrix
    )
    up_blocks, gate_grad, down_grad, down_new, grad_tokens, small_share = tick(
        [last_line],
        (up_blocks, gate_grad, down_grad.astype(full), down_new, grad_tokens, small_share),
    )
    up_grad = join_columns(both_cores(up_blocks), piece)
    last = last_line.sum()
    out_sum = jnp.concatenate([last[in_rows:, : width // 2], last[in_rows:, width // 2 :]], 0)
    last_blocks = [
        jnp.concatenate([wide] + jnp.split(rest, owners // 2, 1), 0)
        for wide, rest in zip(owner_blocks(last[:in_rows], 1), owner_blocks(out_sum, 0))
    ]
    last_halves = both_cores(to_owner(last_blocks))
    in_halves = [part[:, :in_rows] for part in last_halves]
    out_halves = [
        jnp.concatenate(jnp.split(part[:, in_rows:], owners // 2, 1), 2) for part in last_halves
    ]
    out_grad = join_rows(out_halves, sub)
    in_grad = join_columns(in_halves, sub)
    grad_w_down = down_grad
    grad_w_out = out_grad.astype(full)

    def turned(grad_t):
        return lax.optimization_barrier(grad_t.T)

    def my_rows(grad_t):
        count = grad_t.shape[0] // groups
        return turned(lax.dynamic_slice_in_dim(grad_t, group * count, count, 0))

    grad_w_gate = turned(gate_grad).astype(full)
    grad_w_up = turned(up_grad).astype(full)
    grad_w_in = turned(in_grad).astype(full)

    out_shard = lax.dynamic_slice_in_dim(out_grad, group * thin, thin, 1)
    gate_shard = my_rows(gate_grad)
    up_shard = my_rows(up_grad)
    in_shard = my_rows(in_grad)

    for bit in range(groups.bit_length() - 1):
        route = [(i, i ^ (1 << bit)) for i in range(groups)]
        small_share = small_share + lax.ppermute(small_share, "grp", route)
    grad_conv_w = small_share[:taps]
    grad_gain = small_share[taps]
    grad_gain_two = small_share[taps + 1]

    new_w_in, new_moment_in, new_square_in = apply_adam(
        w_in, moment_in, square_in, in_shard.astype(full), rate_matrix, decay_matrix
    )
    new_w_out, new_moment_out, new_square_out = apply_adam(
        w_out, moment_out, square_out, out_shard.astype(full), rate_matrix, decay_matrix
    )
    new_w_gate, new_moment_gate, new_square_gate = apply_adam(
        w_gate, moment_gate, square_gate, gate_shard.astype(full), rate_matrix, decay_matrix
    )
    new_w_up, new_moment_up, new_square_up = apply_adam(
        w_up, moment_up, square_up, up_shard.astype(full), rate_matrix, decay_matrix
    )
    new_w_down, new_moment_down, new_square_down = down_new
    new_conv_w, new_moment_conv, new_square_conv = apply_adam(
        conv_w, moment_conv, square_conv, grad_conv_w, rate_vector, 0.0
    )
    new_gain, new_moment_gain, new_square_gain = apply_adam(
        gain, moment_gain, square_gain, grad_gain, rate_vector, 0.0
    )
    new_gain_two, new_moment_gain_two, new_square_gain_two = apply_adam(
        gain_two, moment_gain_two, square_gain_two, grad_gain_two, rate_vector, 0.0
    )
    return (
        block_out,
        grad_tokens,
        grad_w_in,
        grad_w_out,
        grad_w_gate,
        grad_w_up,
        grad_w_down,
        grad_conv_w,
        grad_gain,
        grad_gain_two,
        new_w_in,
        new_w_out,
        new_w_gate,
        new_w_up,
        new_w_down,
        new_conv_w,
        new_gain,
        new_gain_two,
        new_moment_in,
        new_moment_out,
        new_moment_gate,
        new_moment_up,
        new_moment_down,
        new_moment_conv,
        new_moment_gain,
        new_moment_gain_two,
        new_square_in,
        new_square_out,
        new_square_gate,
        new_square_up,
        new_square_down,
        new_square_conv,
        new_square_gain,
        new_square_gain_two,
    )


def solution(mesh):
    placed = (
        P(("grp", "own"), None),
        P(("grp", "own"), None),
        P(),
        P("own", "grp"),
        P("own", "grp"),
        P("own", "grp"),
        P("own", "grp"),
        P("own", "grp"),
        P(None, "own"),
        P("own"),
        P("own"),
        P("own", "grp"),
        P("own", "grp"),
        P("own", "grp"),
        P("own", "grp"),
        P("own", "grp"),
        P(None, "own"),
        P("own"),
        P("own"),
        P("own", "grp"),
        P("own", "grp"),
        P("own", "grp"),
        P("own", "grp"),
        P("own", "grp"),
        P(None, "own"),
        P("own"),
        P("own"),
    )

    return jax.shard_map(
        local,
        mesh=mesh,
        in_specs=placed,
        out_specs=(
            P(("grp", "own"), None),
            P(("grp", "own"), None),
            P("own", None),
            P("own", None),
            P("own", None),
            P("own", None),
            P("own", None),
            P(None, "own"),
            P("own"),
            P("own"),
            P("own", "grp"),
            P("own", "grp"),
            P("own", "grp"),
            P("own", "grp"),
            P("own", "grp"),
            P(None, "own"),
            P("own"),
            P("own"),
            P("own", "grp"),
            P("own", "grp"),
            P("own", "grp"),
            P("own", "grp"),
            P("own", "grp"),
            P(None, "own"),
            P("own"),
            P("own"),
            P("own", "grp"),
            P("own", "grp"),
            P("own", "grp"),
            P("own", "grp"),
            P("own", "grp"),
            P(None, "own"),
            P("own"),
            P("own"),
        ),
        check_vma=False,
    )
```

```python
import jax
import jax.numpy as jnp
from jax import lax
from jax.sharding import PartitionSpec as P


SEQ_LEN = 2048


eps_norm = 1e-05
eps_adam = 1e-08
beta_one = 0.9
beta_two = 0.95
train_step = 5
rate_matrix = 0.004
rate_vector = 0.1
decay_matrix = 0.1

half = jnp.bfloat16
full = jnp.float32


def exchange(block, k):
    devices = range(lax.axis_size("own"))
    return lax.ppermute(block, "own", [(i, i ^ k) for i in devices])


def gather_own(block):
    places = range(1, lax.axis_size("own"))
    arrived = [exchange(block, k) for k in places]
    return jnp.concatenate([block] + arrived, 0)


def scatter_own(part_of):
    places = range(1, lax.axis_size("own"))
    arrived = []
    for k in places:
        part = part_of(k).astype(half)
        arrived.append(exchange(part, k))
    total = part_of(0)
    for block in arrived:
        total = total + block.astype(full)
    return total


def passed_along(block, distance):
    devices = range(lax.axis_size("grp"))
    route = [(i - distance, i) for i in devices if i - distance in devices]
    return lax.ppermute(block, "grp", route)


def swap_own(pieces):
    return lax.all_to_all(pieces, "own", 0, 0, tiled=True)


def stream_starts(doc_lengths, seq_len):
    starts = jnp.cumsum(doc_lengths, axis=1) - doc_lengths
    base = (jnp.arange(doc_lengths.shape[0], dtype=jnp.int32) * seq_len)[:, None]
    first = (jnp.arange(doc_lengths.shape[1], dtype=jnp.int32) == 0)[None, :]
    return jnp.where(first, 0, base + starts).reshape(-1)


def since_start(positions, stream):
    below = jnp.where(stream[None, :] <= positions[:, None], stream[None, :], 0)
    return positions - jnp.max(below, axis=1)


def apply_adam(param, first, second, grad, rate, decay):
    first_new = beta_one * first + (1.0 - beta_one) * grad
    second_new = beta_two * second + (1.0 - beta_two) * grad * grad
    first_hat = first_new / (1.0 - beta_one**train_step)
    second_hat = second_new / (1.0 - beta_two**train_step)
    param_new = param - rate * (first_hat / (jnp.sqrt(second_hat) + eps_adam) + decay * param)
    return (param_new, first_new, second_new)


def dot(left, right):
    return jnp.dot(left, right, preferred_element_type=full)


def dot_rows(left, right):
    return lax.dot_general(left, right, (((1,), (1,)), ((), ())), preferred_element_type=full)


def dot_tokens(left, right):
    return lax.dot_general(left, right, (((0,), (0,)), ((), ())), preferred_element_type=full)


def pick(index, blocks):
    total = jnp.zeros_like(blocks[0])
    for place, block in enumerate(blocks):
        total = jnp.where(index == place, block, total)
    return total


def local(
    tokens,
    cotangent,
    doc_lengths,
    w_in,
    w_out,
    w_gate,
    w_up,
    w_down,
    conv_w,
    gain,
    gain_two,
    moment_in,
    moment_out,
    moment_gate,
    moment_up,
    moment_down,
    moment_conv,
    moment_gain,
    moment_gain_two,
    square_in,
    square_out,
    square_gate,
    square_up,
    square_down,
    square_conv,
    square_gain,
    square_gain_two,
):
    groups = lax.axis_size("grp")
    owners = lax.axis_size("own")
    group = lax.axis_index("grp")
    owner = lax.axis_index("own")
    rows, width = tokens.shape
    taps = conv_w.shape[0]
    rim = taps - 1
    channels = width // owners
    sub = width // (groups * owners)
    run = w_gate.shape[1] * groups // owners
    share = groups // owners
    thin = w_out.shape[1]

    def columns_for(matrix, pieces):
        cut = matrix.astype(half).T.reshape(pieces, owners, -1, channels)
        return cut.transpose(1, 0, 2, 3).reshape(owners, -1, channels)

    def rows_for(matrix):
        cut = matrix.astype(half).reshape(share, owners, -1, thin)
        return cut.transpose(1, 2, 0, 3).reshape(owners, -1, channels)

    def columns_from(pieces):
        return pieces.transpose(1, 0, 2).reshape(-1, width)

    def rows_gathered(blocks):
        cut = blocks.reshape(groups, -1, groups, thin)
        return cut.transpose(2, 1, 0, 3).reshape(-1, width)

    small = jnp.concatenate([conv_w, gain[None], gain_two[None]], 0).astype(half)
    small = jnp.broadcast_to(small[None], (owners,) + small.shape)
    small_rows = small.shape[1]
    first = jnp.concatenate([columns_for(w_in, 3), rows_for(w_out), small], 1)
    first = swap_own(first)
    tokens_late, first = lax.optimization_barrier((tokens, first))
    x_half = gather_own(tokens_late)
    split = 3 * sub
    small = first[:, split + sub :].transpose(1, 0, 2).reshape(small_rows, width).astype(full)
    first = lax.all_gather(columns_from(first[:, : split + sub]), "grp", axis=0, tiled=False)
    in_t = first[:, :split].reshape(3 * channels, width)
    out_half = rows_gathered(first[:, split:])
    conv_all = small[:taps].reshape(taps, groups, owners, sub)
    conv_float = lax.dynamic_index_in_dim(conv_all, owner, 2, False).reshape(taps, channels)
    gain_float = small[taps]
    gain_two_float = small[taps + 1]
    second = jnp.concatenate([columns_for(w_gate, 1), columns_for(w_up, 1), rows_for(w_down)], 1)
    piece = run // groups
    second = swap_own(second)
    second = lax.all_gather(columns_from(second), "grp", axis=0, tiled=False)
    gate_t = second[:, :piece].reshape(run, width)
    up_t = second[:, piece : 2 * piece].reshape(run, width)
    down_half = rows_gathered(second[:, 2 * piece :])
    cot_late, x_half = lax.optimization_barrier((cotangent, x_half))
    cot_half = gather_own(cot_late)

    places = [owner ^ k for k in range(owners)]
    stream = stream_starts(doc_lengths, SEQ_LEN)
    line = jnp.arange(rows, dtype=jnp.int32)
    position = jnp.concatenate([(group * owners + place) * rows + line for place in places])
    since = since_start(position, stream).reshape(owners, rows, 1)

    x_all = x_half.astype(full)
    inv_all = lax.rsqrt(jnp.mean(x_all * x_all, axis=1, keepdims=True) + eps_norm)
    normed = (x_all * inv_all * gain_float).astype(half)
    project = dot_rows(normed, in_t)
    b_gate = project[:, :channels].reshape(owners, rows, channels)
    c_gate = project[:, channels : 2 * channels].reshape(owners, rows, channels)
    x_value = project[:, 2 * channels :].reshape(owners, rows, channels)
    gated = b_gate * x_value
    tails = [gated[k, rows - rim :] for k in range(owners)]
    last_tail = pick((owners - 1) ^ owner, tails)
    before_group = passed_along(last_tail, 1)
    before = jnp.stack(
        [
            jnp.where(place == 0, before_group, pick((place - 1) ^ owner, tails))
            for place in places
        ]
    )
    extended = jnp.concatenate([before, gated], 1)

    def moved(tap):
        return extended[:, rim - tap : rim - tap + rows]

    convolved = conv_float[0] * gated
    for tap in range(1, taps):
        convolved = convolved + jnp.where(since >= tap, conv_float[tap] * moved(tap), 0.0)
    mixed = (c_gate * convolved).astype(half)
    x_float = tokens.astype(full)
    middle = x_float + scatter_own(lambda k: dot(mixed[k], out_half))
    inv_two = lax.rsqrt(jnp.mean(middle * middle, axis=1, keepdims=True) + eps_norm)
    normed_two = gather_own((middle * inv_two * gain_two_float).astype(half))
    gate = dot_rows(normed_two, gate_t)
    up = dot_rows(normed_two, up_t)
    sig = jax.nn.sigmoid(gate)
    activated = gate * sig
    hidden = (activated * up).astype(half)

    def scatter_grp(array, tiled):
        return lax.psum_scatter(array, "grp", scatter_dimension=0, tiled=tiled)

    down_part = dot_tokens(cot_half, hidden).astype(half)
    gate, up, down_part = lax.optimization_barrier((gate, up, down_part))
    down_sum = scatter_grp(down_part, True)
    sig = jax.nn.sigmoid(gate)
    activated = gate * sig
    grad_hidden = dot_rows(cot_half, down_half)
    grad_gate = (grad_hidden * up * sig * (1.0 + gate * (1.0 - sig))).astype(half)
    grad_up = (grad_hidden * activated).astype(half)

    def block(array, k):
        return array[k * rows : (k + 1) * rows]

    gate_part = dot_tokens(grad_gate, normed_two).astype(half)
    up_part = dot_tokens(grad_up, normed_two).astype(half)
    pair_part = jnp.concatenate(
        [gate_part.reshape(groups, -1, width), up_part.reshape(groups, -1, width)], 1
    )
    pair_sum = scatter_grp(pair_part, False)

    grad_normed_two = scatter_own(
        lambda k: dot(block(grad_gate, k), gate_t) + dot(block(grad_up, k), up_t),
    )
    gain_two_rows = jnp.sum(grad_normed_two * middle * inv_two, axis=0)
    weighted_two = gain_two_float * grad_normed_two
    grad_middle = (
        cotangent.astype(full)
        + inv_two * weighted_two
        - middle
        * inv_two
        * inv_two
        * inv_two
        * jnp.mean(weighted_two * middle, axis=1, keepdims=True)
    )
    grad_middle_half = gather_own(grad_middle.astype(half))
    grad_mixed = dot_rows(grad_middle_half, out_half).reshape(owners, rows, channels)
    grad_c = grad_mixed * convolved
    grad_conv = grad_mixed * c_gate
    tap_sums = [jnp.sum(grad_conv * gated, axis=(0, 1))]
    grad_gated = conv_float[0] * grad_conv
    kept = [jnp.where(since >= tap, grad_conv, 0.0) for tap in range(1, taps)]
    heads = [
        jnp.concatenate([kept[tap - 1][k, :tap] for tap in range(1, taps)], 0)
        for k in range(owners)
    ]
    after_group = passed_along(pick(owner, heads), -1)
    after = jnp.stack(
        [
            jnp.where(place == owners - 1, after_group, pick((place + 1) ^ owner, heads))
            for place in places
        ]
    )
    line = 0
    for tap in range(1, taps):
        ahead = jnp.concatenate([kept[tap - 1][:, tap:], after[:, line : line + tap]], 1)
        line = line + tap
        grad_gated = grad_gated + conv_float[tap] * ahead
        tap_sums.append(jnp.sum(kept[tap - 1] * moved(tap), axis=(0, 1)))
    grad_project = (
        jnp.concatenate([grad_gated * x_value, grad_c, grad_gated * b_gate], 2)
        .astype(half)
        .reshape(owners * rows, 3 * channels)
    )
    in_part = dot_tokens(grad_project, normed).astype(half).reshape(groups, -1, width)
    out_part = dot_tokens(grad_middle_half, mixed.reshape(owners * rows, channels)).astype(half)
    out_part = out_part.reshape(groups, owners, -1, channels).transpose(0, 2, 1, 3)
    last_part = jnp.concatenate([in_part, out_part.reshape(groups, -1, width)], 1)
    last_sum = scatter_grp(last_part, False)

    def columns_shard(pieces, parts):
        cut = pieces.reshape(owners, parts, -1, channels)
        return cut.transpose(1, 0, 2, 3).reshape(-1, channels)

    def rows_shard(pieces):
        cut = pieces.reshape(owners, -1, share, thin)
        return cut.transpose(2, 0, 1, 3).reshape(-1, thin)

    piece = run // groups
    pair = pair_sum.reshape(-1, owners, channels).transpose(1, 0, 2)
    down_rows = down_sum.T.reshape(owners, share, piece, thin).transpose(0, 2, 1, 3)
    big = jnp.concatenate([pair, down_rows.reshape(owners, piece, channels)], 1)
    big = swap_own(big)
    big, hidden_late, project_late = lax.optimization_barrier((big, hidden, grad_project))
    gate_shard = big[:, :piece].reshape(owners * piece, channels)
    up_shard = big[:, piece : 2 * piece].reshape(owners * piece, channels)
    down_shard = rows_shard(big[:, 2 * piece :])
    big_all = jnp.concatenate(
        [gate_shard, up_shard, big[:, 2 * piece :].reshape(-1, channels)], 0
    )
    big_all = lax.all_gather(big_all, "grp", axis=0, tiled=False)
    split = 3 * sub
    in_rows = last_sum[:split].reshape(split, owners, channels).transpose(1, 0, 2)
    out_rows = last_sum[split:].reshape(-1, owners, channels).transpose(1, 0, 2)
    out_rows = out_rows.reshape(thin, channels).T.reshape(owners, share, sub, thin)
    out_rows = out_rows.transpose(0, 2, 1, 3).reshape(owners, sub, channels)
    last = jnp.concatenate([in_rows, out_rows], 1)
    last = swap_own(last)
    in_shard = columns_shard(last[:, :split], 3)
    out_shard = rows_shard(last[:, split:])
    last_all = jnp.concatenate([in_shard, last[:, split:].reshape(-1, channels)], 0)
    last_all = lax.all_gather(last_all, "grp", axis=0, tiled=False)
    grad_normed = scatter_own(lambda k: dot(block(project_late, k), in_t))
    feed_out = scatter_own(lambda k: dot(block(hidden_late, k), down_half))
    block_out = (middle + feed_out).astype(half)
    inv_rms = lax.rsqrt(jnp.mean(x_float * x_float, axis=1, keepdims=True) + eps_norm)
    gain_rows = jnp.sum(grad_normed * x_float * inv_rms, axis=0)
    weighted = gain_float * grad_normed
    grad_tokens = (
        grad_middle
        + inv_rms * weighted
        - x_float
        * inv_rms
        * inv_rms
        * inv_rms
        * jnp.mean(weighted * x_float, axis=1, keepdims=True)
    ).astype(half)
    tap_pieces = jnp.stack(tap_sums).reshape(taps, owners, share * sub).transpose(1, 0, 2)
    tap_pieces = jnp.pad(tap_pieces, ((0, 0), (0, 0), (0, channels - share * sub)))
    gain_pieces = jnp.stack([gain_rows, gain_two_rows]).reshape(2, owners, channels)
    pieces = jnp.concatenate([tap_pieces, gain_pieces.transpose(1, 0, 2)], 1)
    pieces = swap_own(pieces)
    tap_share = pieces[:, :taps, : share * sub].reshape(owners, taps, share, sub)
    tap_share = tap_share.transpose(1, 2, 0, 3).reshape(taps, channels)
    gain_share = jnp.sum(pieces[:, taps:], axis=0)
    small_share = jnp.concatenate([tap_share, gain_share], 0)
    for bit in range(groups.bit_length() - 1):
        route = [(i, i ^ (1 << bit)) for i in range(groups)]
        small_share = small_share + lax.ppermute(small_share, "grp", route)

    def turned(grad_t):
        return lax.optimization_barrier(grad_t.T)

    def new_columns(shard_t, param, first, second):
        shard = turned(shard_t).astype(full)
        return apply_adam(param, first, second, shard, rate_matrix, decay_matrix)

    def new_rows(shard, param, first, second):
        return apply_adam(param, first, second, shard.astype(full), rate_matrix, decay_matrix)

    gate_new = new_columns(gate_shard, w_gate, moment_gate, square_gate)
    up_new = new_columns(up_shard, w_up, moment_up, square_up)
    down_new = new_rows(down_shard, w_down, moment_down, square_down)

    new_w_in, new_moment_in, new_square_in = new_columns(in_shard, w_in, moment_in, square_in)
    new_w_out, new_moment_out, new_square_out = new_rows(
        out_shard, w_out, moment_out, square_out
    )
    new_w_gate, new_moment_gate, new_square_gate = gate_new
    new_w_up, new_moment_up, new_square_up = up_new
    new_w_down, new_moment_down, new_square_down = down_new

    def rows_whole(blocks):
        cut = blocks.reshape(groups, -1, share, thin).transpose(2, 1, 0, 3)
        return cut.reshape(-1, width).astype(full)

    fan = 3 * width // groups
    grad_w_in = turned(last_all[:, :fan].reshape(-1, channels)).astype(full)
    grad_w_out = rows_whole(last_all[:, fan:])
    count = owners * piece
    grad_w_gate = turned(big_all[:, :count].reshape(-1, channels)).astype(full)
    grad_w_up = turned(big_all[:, count : 2 * count].reshape(-1, channels)).astype(full)
    grad_w_down = rows_whole(big_all[:, 2 * count :])
    grad_conv_w = small_share[:taps]
    grad_gain = small_share[taps]
    grad_gain_two = small_share[taps + 1]

    new_conv_w, new_moment_conv, new_square_conv = apply_adam(
        conv_w, moment_conv, square_conv, grad_conv_w, rate_vector, 0.0
    )
    new_gain, new_moment_gain, new_square_gain = apply_adam(
        gain, moment_gain, square_gain, grad_gain, rate_vector, 0.0
    )
    new_gain_two, new_moment_gain_two, new_square_gain_two = apply_adam(
        gain_two, moment_gain_two, square_gain_two, grad_gain_two, rate_vector, 0.0
    )
    return (
        block_out,
        grad_tokens,
        grad_w_in,
        grad_w_out,
        grad_w_gate,
        grad_w_up,
        grad_w_down,
        grad_conv_w,
        grad_gain,
        grad_gain_two,
        new_w_in,
        new_w_out,
        new_w_gate,
        new_w_up,
        new_w_down,
        new_conv_w,
        new_gain,
        new_gain_two,
        new_moment_in,
        new_moment_out,
        new_moment_gate,
        new_moment_up,
        new_moment_down,
        new_moment_conv,
        new_moment_gain,
        new_moment_gain_two,
        new_square_in,
        new_square_out,
        new_square_gate,
        new_square_up,
        new_square_down,
        new_square_conv,
        new_square_gain,
        new_square_gain_two,
    )


def solution(mesh):
    placed = (
        P(("grp", "own"), None),
        P(("grp", "own"), None),
        P(),
        P("own", "grp"),
        P("own", "grp"),
        P("own", "grp"),
        P("own", "grp"),
        P("own", "grp"),
        P(None, "own"),
        P("own"),
        P("own"),
        P("own", "grp"),
        P("own", "grp"),
        P("own", "grp"),
        P("own", "grp"),
        P("own", "grp"),
        P(None, "own"),
        P("own"),
        P("own"),
        P("own", "grp"),
        P("own", "grp"),
        P("own", "grp"),
        P("own", "grp"),
        P("own", "grp"),
        P(None, "own"),
        P("own"),
        P("own"),
    )

    return jax.shard_map(
        local,
        mesh=mesh,
        in_specs=placed,
        out_specs=(
            P(("grp", "own"), None),
            P(("grp", "own"), None),
            P("own", None),
            P("own", None),
            P("own", None),
            P("own", None),
            P("own", None),
            P(None, "own"),
            P("own"),
            P("own"),
            P("own", "grp"),
            P("own", "grp"),
            P("own", "grp"),
            P("own", "grp"),
            P("own", "grp"),
            P(None, "own"),
            P("own"),
            P("own"),
            P("own", "grp"),
            P("own", "grp"),
            P("own", "grp"),
            P("own", "grp"),
            P("own", "grp"),
            P(None, "own"),
            P("own"),
            P("own"),
            P("own", "grp"),
            P("own", "grp"),
            P("own", "grp"),
            P("own", "grp"),
            P("own", "grp"),
            P(None, "own"),
            P("own"),
            P("own"),
        ),
        check_vma=False,
    )
```
